32 devices in a mesh: rep: 8 (over z, y), shard: 4 (over x, core).
Axes of the slice: x: 2, y: 2, z: 4, core: 2. Of those that a mesh axis runs over, the one named last changes fastest.
Arguments:
- tokens: bfloat16 [8192, 1280], P(('rep', 'shard')), may hold values from -6 to 6
- teacher: bfloat16 [8192, 1280], P(('rep', 'shard')), may hold values from -6 to 6
- cotangent: bfloat16 [8192, 1280], P(('rep', 'shard')), may hold values from -6 to 6
- lengths: int32 [8, 3], P('rep'), may hold values from 0 to 1024, as said below
- balance: int32 [8, 1024], P('rep'), may hold values from 0 to 1023, each once within a row
- qkv_weight: bfloat16 [2, 1280, 3840], P(None, 'shard'), may hold values from -0.15625 to 0.15625
- out_weight: bfloat16 [2, 1280, 1280], P(None, 'shard'), may hold values from -0.625 to 0.625
- up_weight: bfloat16 [2, 1280, 1280], P(None, 'shard'), may hold values from -0.15625 to 0.15625
- down_weight: bfloat16 [2, 1280, 1280], P(None, 'shard'), may hold values from -0.15625 to 0.15625
- gains: bfloat16 [2, 2, 1280], P(None, None, 'shard'), may hold values from 0.099609375 to 1.8984375
- query_scale: bfloat16 [2, 80], P(None, 'shard'), may hold values from -1.5 to 1.5
Outputs:
- layer_output: bfloat16 [8192, 1280], P(('rep', 'shard'))
- input_grad: float32 [8192, 1280], P(('rep', 'shard'))
- grad_qkv: float32 [2, 1280, 3840], P(None, 'shard')
- grad_out: float32 [2, 1280, 1280], P(None, 'shard')
- grad_up: float32 [2, 1280, 1280], P(None, 'shard')
- grad_down: float32 [2, 1280, 1280], P(None, 'shard')
- grad_gains: float32 [2, 2, 1280], P(None, None, 'shard')
- grad_scale: float32 [2, 80], P(None, 'shard')
The draws below stay inside these ranges and needn't reach their ends.
Inputs may be any that keep to these rules, and one draw needn't show every extreme that they name: Row r lists the lengths of the sequences that fill pack r from position 0 in order; positions after their sum are padding. Lengths may be zero; row 0 is a single sequence of 1024 tokens. `balance`: each row is a permutation of the positions of one pack.
All inputs are finite; a program needn't handle non-finite values.
Results may differ from the reference program's by a relative error of at most 0.018.
Values may be sent and summed in bfloat16 or wider, within the bound.
No kernel may reach another device: no remote copies, remote signals or barrier semaphores. Data moves between devices by JAX's collectives and lax.ppermute only.
A program may use at most 320 MiB of HBM per device.

```python
import math
import jax
import jax.numpy as jnp
from jax import lax

D = 1280
HEADS = 16
HDIM = 80
FF = 1280
LAYERS = 2
SLOTS = 3
PACK = 1024
TOKENS = 8192
N_REP = 8


def draw_lengths(key, part):
    group_ids = jnp.arange(N_REP, dtype=jnp.int32)
    cut_key = jax.random.fold_in(key, 11)
    drop_key = jax.random.fold_in(key, 12)
    trend_total = PACK - 2 * PACK * group_ids // (3 * max(N_REP - 1, 1))
    jitter_drop = jax.random.randint(drop_key, (N_REP,), 0, PACK // 8 + 1, dtype=jnp.int32)
    live_total = jnp.where(group_ids == 0, PACK, trend_total - jitter_drop).astype(jnp.int32)
    raw_cuts = jax.random.randint(cut_key, (N_REP, SLOTS - 1), 0, PACK + 1, dtype=jnp.int32)
    cut_points = jnp.sort(raw_cuts * live_total[:, None] // PACK, axis=1)
    edge_list = jnp.concatenate([jnp.zeros((N_REP, 1), jnp.int32), cut_points, live_total[:, None]], axis=1)
    seq_lengths = edge_list[:, 1:] - edge_list[:, :-1]
    single_row = jnp.zeros((SLOTS,), jnp.int32).at[0].set(PACK)
    return jnp.where(group_ids[:, None] == 0, single_row[None, :], seq_lengths).astype(jnp.int32)


def block_scale(rng, dims, cuts, smallest, high):
    factor_of = 1.0
    for axis_at, parts in cuts:
        steps = jax.random.uniform(jax.random.fold_in(jax.random.fold_in(rng, 6), axis_at), (parts,), jnp.float32, smallest / len(cuts), high / len(cuts))
        factor_of = factor_of * jnp.repeat(jnp.exp(steps), dims[axis_at] // parts).reshape((-1,) + (1,) * (len(dims) - 1 - axis_at))
    return factor_of


def gaussian(own_key, extent, width, reach, shards=(), held_as=jnp.bfloat16):
    level = block_scale(own_key, extent, shards, -0.22, 0.18) if shards else 1.0
    values = jax.random.normal(own_key, extent, jnp.float32) * width * level
    return jnp.minimum(jnp.maximum(values, -reach), reach).astype(held_as)


def setup_inputs(seed: int = 0) -> dict:
    seeds = jax.random.split(jax.random.key(seed), 12)
    return {
        "tokens": gaussian(seeds[0], (TOKENS, D), 1.0, 6.0, ((0, 32),)),
        "teacher": gaussian(seeds[1], (TOKENS, D), 1.0, 6.0, ((0, 32),)),
        "cotangent": gaussian(seeds[2], (TOKENS, D), 1.0, 6.0, ((0, 32),)),
        "lengths": draw_lengths(jax.random.fold_in(seeds[11], 71), 0),
        "balance": jax.vmap(lambda own: jax.random.permutation(own, PACK))(jax.random.split(seeds[4], N_REP)).reshape((N_REP, PACK)).astype(jnp.int32),
        "qkv_weight": gaussian(seeds[5], (LAYERS, D, 3 * D), D ** -0.5, 0.15625, ((1, 4),)),
        "out_weight": gaussian(seeds[6], (LAYERS, D, D), (D // 16) ** -0.5, 0.625, ((1, 4),)),
        "up_weight": gaussian(seeds[7], (LAYERS, D, FF), D ** -0.5, 0.15625, ((1, 4),)),
        "down_weight": gaussian(seeds[8], (LAYERS, FF, D), FF ** -0.5, 0.15625, ((1, 4),)),
        "gains": jnp.clip(1.0 + 0.18 * jax.random.normal(seeds[9], (LAYERS, 2, D), jnp.float32), 0.099609375, 1.8984375).astype(jnp.bfloat16),
        "query_scale": jnp.clip(jax.random.uniform(seeds[10], (LAYERS, HDIM), jnp.float32, -1.5, 1.5) * block_scale(seeds[10], (LAYERS, HDIM), ((1, 4),), -0.4, 0.0), -1.5, 1.5).astype(jnp.bfloat16),
    }


@jax.custom_vjp
def low(v):
    return lax.optimization_barrier(v.astype(jnp.bfloat16)).astype(jnp.float32)

@jax.custom_vjp
def low_back(v):
    return v

def low_keep(v):
    return (low(v), None)

def low_pass(kept, grad):
    return (grad,)

def back_keep(v):
    return (v, None)

def back_low(kept, grad):
    return (low(grad),)
low.defvjp(low_keep, low_pass)
low_back.defvjp(back_keep, back_low)
eps = 1e-06
scale_base = 1.442695
highest = lax.Precision.HIGHEST

def hdot(left, right):
    return jnp.dot(left, right, precision=highest)

def root_norm(values, gain):
    return values * lax.rsqrt(lax.optimization_barrier(jnp.mean(values * values, axis=-1, keepdims=True)) + eps) * gain

def attention(queries, keys_all, values_all, allowed):
    pack_size = queries.shape[0]

    def split_heads(matrix):
        return matrix.reshape(pack_size, HEADS, HDIM).transpose(1, 0, 2)

    def one_head(pieces):
        query_head, key_head, value_head = pieces
        scores = low_back(hdot(query_head, key_head.T))
        scores = jnp.where(allowed, scores, -1e+30)
        top_score = lax.optimization_barrier(jnp.max(scores, axis=-1, keepdims=True))
        weights = jnp.exp(scores - top_score)
        probs = weights / lax.optimization_barrier(jnp.sum(weights, axis=-1, keepdims=True))
        return hdot(low(probs), value_head)
    context = lax.map(jax.checkpoint(one_head), (split_heads(queries), split_heads(keys_all), split_heads(values_all)))
    return context.transpose(1, 0, 2).reshape(pack_size, HEADS * HDIM)

def layer_forward(current, w_qkv, w_out, w_up, w_down, gain_pair, scale_raw, allowed):
    first_low = low(root_norm(current, gain_pair[0]))
    mixed = low_back(hdot(first_low, w_qkv))
    head_scale = jnp.tile(scale_base / math.sqrt(HDIM) * jnp.log1p(jnp.exp(scale_raw)), HEADS)
    queries = low(mixed[:, :D] * head_scale)
    keys_low = low(mixed[:, D:2 * D])
    values_low = low(mixed[:, 2 * D:])
    context = attention(queries, keys_low, values_low, allowed)
    context_low = low(low_back(context))
    after_attn = current + low_back(hdot(context_low, w_out))
    second_low = low(root_norm(after_attn, gain_pair[1]))
    pre_act = low_back(hdot(second_low, w_up))
    hidden_low = low(pre_act * jax.nn.sigmoid(pre_act))
    return after_attn + low_back(hdot(hidden_low, w_down))

def forward(current, qkv_all, out_all, up_all, down_all, gain_all, scale_all, allowed):
    for layer_id in range(LAYERS):
        current = layer_forward(current, qkv_all[layer_id], out_all[layer_id], up_all[layer_id], down_all[layer_id], gain_all[layer_id], scale_all[layer_id], allowed)
    return current

def reference(tokens, teacher, cotangent, lengths, balance, qkv_weight, out_weight, up_weight, down_weight, gains, query_scale):
    params = (qkv_weight.astype(jnp.float32), out_weight.astype(jnp.float32), up_weight.astype(jnp.float32), down_weight.astype(jnp.float32), gains.astype(jnp.float32), query_scale.astype(jnp.float32))
    loss_scale = N_REP * PACK / jnp.sum(lengths).astype(jnp.float32)
    positions = jnp.arange(PACK, dtype=jnp.int32)

    def one_group(totals, item):
        rows_in, targets, cot_rows, seq_lens, balance_row = item
        seq_ends = jnp.cumsum(seq_lens)
        live_count = seq_ends[-1]
        segment = lax.optimization_barrier(jnp.sum((positions[:, None] >= seq_ends[None, :]).astype(jnp.int32), axis=1))
        segment = jnp.where(positions < live_count, segment, SLOTS + positions)
        allowed = (segment[:, None] == segment[None, :]) & (positions[None, :] <= positions[:, None])
        inverse = jnp.argsort(balance_row).astype(jnp.int32)
        aligned = jnp.take(targets, inverse, axis=0)
        valid = (positions < live_count).astype(jnp.float32)[:, None]

        def run(current, qkv_all, out_all, up_all, down_all, gain_all, scale_all):
            return forward(current, qkv_all, out_all, up_all, down_all, gain_all, scale_all, allowed)
        output, pullback = jax.vjp(run, rows_in, params[0], params[1], params[2], params[3], params[4], params[5])
        grads = pullback(cot_rows + loss_scale * valid * (output - aligned))
        totals = tuple((left + right for left, right in zip(totals, grads[1:])))
        return (totals, (output.astype(jnp.bfloat16), grads[0]))
    zeros = tuple((jnp.zeros_like(param) for param in params))
    items = (tokens.astype(jnp.float32).reshape(N_REP, PACK, D), teacher.astype(jnp.float32).reshape(N_REP, PACK, D), cotangent.astype(jnp.float32).reshape(N_REP, PACK, D), lengths, balance)
    totals, (outputs, input_grads) = lax.scan(one_group, zeros, items)
    return (outputs.reshape(N_REP * PACK, D), input_grads.reshape(N_REP * PACK, D), totals[0], totals[1], totals[2], totals[3], totals[4], totals[5])
```

```python
import functools
import math

import jax
import jax.numpy as jnp
from jax import lax
from jax.experimental import pallas as pl
from jax.experimental.pallas import tpu as pltpu
from jax.sharding import PartitionSpec as P

HDIM = 80
LAYERS = 2
eps = 1e-06
scale_base = 1.442695
masked_score = -1e30
f32 = jnp.float32
bf16 = jnp.bfloat16


VM = pl.BlockSpec(memory_space=pltpu.VMEM)
ANY = pl.BlockSpec(memory_space=pl.ANY)
SM = pl.BlockSpec(memory_space=pltpu.SMEM)


def nn(a, b):
    return lax.dot_general(a, b, (((1,), (0,)), ((), ())), preferred_element_type=f32)


def nt(a, b):
    return lax.dot_general(a, b, (((1,), (1,)), ((), ())), preferred_element_type=f32)


def tn(a, b):
    return lax.dot_general(a, b, (((0,), (0,)), ((), ())), preferred_element_type=f32)


def sds(shape, dtype):
    return jax.ShapeDtypeStruct(shape, dtype)


def call(kernel, ins, specs, outs, scratch=(), flops=0, limit=None, name=None):
    moved = sum(math.prod(x.shape) * x.dtype.itemsize for x in ins)
    moved += sum(math.prod(x.shape) * x.dtype.itemsize for x in outs)
    return pl.pallas_call(
        kernel,
        out_shape=tuple(outs),
        in_specs=list(specs),
        out_specs=tuple([VM] * len(outs)),
        scratch_shapes=list(scratch),
        cost_estimate=pl.CostEstimate(flops=int(flops), bytes_accessed=int(moved), transcendentals=0),
        compiler_params=pltpu.CompilerParams(vmem_limit_bytes=limit),
        name=name,
    )(*ins)


def rows_of(e, size):
    return pl.ds(pl.multiple_of(e * size, size), size)


def inv_root(v):
    return lax.rsqrt(jnp.mean(v * v, axis=-1, keepdims=True) + eps)


def norm_back(v, gain, grad):
    r = inv_root(v)
    scaled = grad * gain
    inner = jnp.mean(scaled * v, axis=-1, keepdims=True)
    return r * scaled - v * (r * r * r) * inner, jnp.sum(grad * v * r, axis=0, keepdims=True)


def qkv_first_kernel(d_ref, a0, a1, hs, w0, w1, w2, w3, o0, o1, w_out, sems):
    d = d_ref[0]
    depth = w0.shape[0]
    copies = [
        pltpu.make_async_copy(w, w_out.at[rows_of(d ^ j, depth), :], sems.at[j])
        for j, w in enumerate((w0, w1, w2, w3))
    ]
    for c in copies:
        c.start()
    for c in copies:
        c.wait()
    width = hs.shape[1]
    for a, o in ((a0, o0), (a1, o1)):
        m = nn(a[...], w_out[...])
        o[:, :width] = (m[:, :width] * hs[...]).astype(bf16)
        o[:, width:] = m[:, width:].astype(bf16)


def qkv_second_kernel(a0, a1, hs, w, o0, o1):
    width = hs.shape[1]
    for a, o in ((a0, o0), (a1, o1)):
        m = nn(a[...], w[...])
        o[:, :width] = (m[:, :width] * hs[...]).astype(bf16)
        o[:, width:] = m[:, width:].astype(bf16)


def split_in(d, blocks, q_s, k_s, v_s):
    heads, _, hd = q_s.shape
    rows = blocks[0].shape[0]
    width = heads * hd
    for j, blk in enumerate(blocks):
        at = rows_of(d ^ j, rows)
        for t in range(heads):
            q_s[t, at, :] = blk[:, t * hd : (t + 1) * hd]
            k_s[t, at, :] = blk[:, width + t * hd : width + (t + 1) * hd]
            v_s[t, at, :] = blk[:, 2 * width + t * hd : 2 * width + (t + 1) * hd]


def scores_t(k, q_i, start_i, lo, n):
    s = nt(k, q_i)
    width = q_i.shape[0]
    kpos = lax.broadcasted_iota(jnp.int32, (n, width), 0)
    qpos = lo + lax.broadcasted_iota(jnp.int32, (n, width), 1)
    return jnp.where((kpos >= start_i) & (kpos <= qpos), s, masked_score)


def attend_kernel(d_ref, b0, b1, b2, b3, start, c0, c1, c2, c3, lse, q_s, k_s, v_s, ct_s):
    d = d_ref[0]
    heads, pack, hd = q_s.shape
    rows = b0.shape[0]
    split_in(d, (b0, b1, b2, b3), q_s, k_s, v_s)

    def one_head(t, carry):
        v_t = v_s[t].T
        for i in range(pack // rows):
            lo = i * rows
            n = lo + rows
            s = scores_t(k_s[t, :n, :], q_s[t, lo:n, :], start[:, lo:n], lo, n)
            top = jnp.max(s, axis=0, keepdims=True)
            p = jnp.exp(s - top)
            total = jnp.sum(p, axis=0, keepdims=True)
            ctx = nn(v_t[:, :n], p.astype(bf16)) / total
            ct_s[pl.ds(pl.multiple_of(t * hd, hd), hd), lo:n] = ctx
            lse[pl.ds(t, 1), lo:n] = top + jnp.log(total)
        return carry

    lax.fori_loop(0, heads, one_head, 0)
    for j, c in enumerate((c0, c1, c2, c3)):
        c[...] = ct_s[:, rows_of(d ^ j, rows)].T.astype(bf16)


def attend_back_kernel(
    d_ref, g0, g1, g2, g3, w_out, b0, b1, b2, b3, c0, c1, c2, c3, lse, start, hs,
    m0, m1, m2, m3, gs_sum, q_s, k_s, v_s, gc_s, d_s, gqt_s, gk_s, gv_s,
):
    d = d_ref[0]
    heads, pack, hd = q_s.shape
    rows = b0.shape[0]
    width = heads * hd
    blocks = (b0, b1, b2, b3)
    split_in(d, blocks, q_s, k_s, v_s)
    for j, (g, c) in enumerate(((g0, c0), (g1, c1), (g2, c2), (g3, c3))):
        at = rows_of(d ^ j, rows)
        gc = nt(g[...], w_out[...]).astype(bf16)
        prod = (gc.astype(f32) * c[...].astype(f32)).T
        for t in range(heads):
            gc_s[t, at, :] = gc[:, t * hd : (t + 1) * hd]
            d_s[t : t + 1, at] = jnp.sum(prod[t * hd : (t + 1) * hd, :], axis=0, keepdims=True)
    gk_s[...] = jnp.zeros_like(gk_s)
    gv_s[...] = jnp.zeros_like(gv_s)

    def one_head(t, carry):
        k_t = k_s[t].T
        for i in range(pack // rows):
            lo = i * rows
            n = lo + rows
            q_i = q_s[t, lo:n, :]
            gc_i = gc_s[t, lo:n, :]
            s = scores_t(k_s[t, :n, :], q_i, start[:, lo:n], lo, n)
            p = jnp.exp(s - lse[pl.ds(t, 1), lo:n])
            dp = nt(v_s[t, :n, :], gc_i)
            gs = (p * (dp - d_s[pl.ds(t, 1), lo:n])).astype(bf16)
            gv_s[t, :n, :] += nn(p.astype(bf16), gc_i)
            gk_s[t, :n, :] += nn(gs, q_i)
            gqt_s[pl.ds(pl.multiple_of(t * hd, hd), hd), lo:n] = nn(k_t[:, :n], gs)
        return carry

    lax.fori_loop(0, heads, one_head, 0)
    total = jnp.zeros((1, width), f32)
    for j, (m, blk) in enumerate(((m0, b0), (m1, b1), (m2, b2), (m3, b3))):
        at = rows_of(d ^ j, rows)
        gq = gqt_s[:, at].T
        total = total + jnp.sum(gq * blk[:, :width].astype(f32), axis=0, keepdims=True)
        m[:, :width] = (gq * hs[...]).astype(bf16)
        m[:, width : 2 * width] = jnp.concatenate([gk_s[t, at, :] for t in range(heads)], axis=1).astype(bf16)
        m[:, 2 * width :] = jnp.concatenate([gv_s[t, at, :] for t in range(heads)], axis=1).astype(bf16)
    gs_sum[...] = total


def ffn_kernel(
    d_ref, c0, c1, c2, c3, h, g2, gn, wo0, wo1, wo2, wo3, wu0, wu1, wu2, wu3, wd0, wd1, wd2, wd3,
    h1_o, u_o, bb_o, hb_o, y_o, ab_o, wo_s, wu_s, wd_s, sems,
):
    d = d_ref[0]
    depth = wo0.shape[0]
    groups = []
    for m, (pieces, scr) in enumerate(
        (((wo0, wo1, wo2, wo3), wo_s), ((wu0, wu1, wu2, wu3), wu_s), ((wd0, wd1, wd2, wd3), wd_s))
    ):
        groups.append([
            pltpu.make_async_copy(w, scr.at[rows_of(d ^ j, depth), :], sems.at[m, j])
            for j, w in enumerate(pieces)
        ])
    for group in groups:
        for c in group:
            c.start()
    for c in groups[0]:
        c.wait()
    h1 = h[...].astype(f32)
    for j, c in enumerate((c0, c1, c2, c3)):
        h1 = h1 + nn(c[...], wo_s[rows_of(d ^ j, depth), :])
    h1_o[...] = h1
    bb = (h1 * inv_root(h1) * g2[...]).astype(bf16)
    bb_o[...] = bb
    for c in groups[1]:
        c.wait()
    u = nn(bb, wu_s[...])
    u_o[...] = u
    hb = (u / (1.0 + jnp.exp(-u))).astype(bf16)
    hb_o[...] = hb
    for c in groups[2]:
        c.wait()
    y = h1_o[...] + nn(hb, wd_s[...])
    y_o[...] = y
    ab_o[...] = (y * inv_root(y) * gn[...]).astype(bf16)


def ffn_back_kernel(
    d_ref, g, h1, u_r, g2, wu0, wu1, wu2, wu3, wd0, wd1, wd2, wd3,
    gm_o, gu_o, g1_o, go_o, dg_o, wu_s, wd_s, sems,
):
    d = d_ref[0]
    depth = wu0.shape[0]
    groups = []
    for m, (pieces, scr) in enumerate((((wd0, wd1, wd2, wd3), wd_s), ((wu0, wu1, wu2, wu3), wu_s))):
        groups.append([
            pltpu.make_async_copy(w, scr.at[rows_of(d ^ j, depth), :], sems.at[m, j])
            for j, w in enumerate(pieces)
        ])
    for group in groups:
        for c in group:
            c.start()
    gm = g[...].astype(bf16)
    gm_o[...] = gm
    for c in groups[0]:
        c.wait()
    gh = nt(gm, wd_s[...])
    u = u_r[...]
    s = 1.0 / (1.0 + jnp.exp(-u))
    gu = (gh * s * (1.0 + u * (1.0 - s))).astype(bf16)
    gu_o[...] = gu
    for c in groups[1]:
        c.wait()
    gb = nt(gu, wu_s[...])
    back, dg = norm_back(h1[...], g2[...], gb)
    g1 = g[...] + back
    g1_o[...] = g1
    go_o[...] = g1.astype(bf16)
    dg_o[...] = dg


def ffn_grad_kernel(d_ref, hb, gm, bb, gu, keep, send, acc):
    d = d_ref[0]
    depth = keep.shape[1]
    for m, (left, right) in enumerate(((bb, gu), (hb, gm))):
        acc[...] = tn(left[...], right[...])
        for j in range(4):
            to = keep if j % 2 == 0 else send
            to[2 * m + j // 2] = acc[rows_of(d ^ j, depth), :].astype(bf16)


def split_add_kernel(a, b, keep, send):
    for m in range(a.shape[0] // 2):
        keep[m] = (a[2 * m].astype(f32) + b[2 * m].astype(f32)).astype(bf16)
        send[m] = (a[2 * m + 1].astype(f32) + b[2 * m + 1].astype(f32)).astype(bf16)


def half_add_kernel(y_ref, a, b, keep, send):
    half = keep.shape[1]
    y = y_ref[0]
    for m in range(a.shape[0]):
        for to, which in ((keep, y), (send, 1 - y)):
            at = rows_of(which, half)
            to[m] = (a[m, at, :].astype(f32) + b[m, at, :].astype(f32)).astype(bf16)


def ga_kernel(m0, m1, m2, m3, w, keep, send):
    send[0] = nt(m1[...], w[...]).astype(bf16)
    send[1] = nt(m3[...], w[...]).astype(bf16)
    keep[0] = nt(m0[...], w[...]).astype(bf16)
    keep[1] = nt(m2[...], w[...]).astype(bf16)


def attn_grad_kernel(
    d_ref, y_ref, a0, a1, a2, a3, m0, m1, m2, m3, c0, c1, c2, c3, g0, g1, g2, g3,
    qk, qs, ok, os, acc, acc_o,
):
    d = d_ref[0]
    y = y_ref[0]
    half = qk.shape[1]
    acc[...] = tn(a0[...], m0[...])
    for a, m in ((a1, m1), (a2, m2), (a3, m3)):
        acc[...] += tn(a[...], m[...])
    for j in range(4):
        base = (d ^ j) * (2 * half)
        for to, which in ((qk, y), (qs, 1 - y)):
            at = pl.ds(pl.multiple_of(base + which * half, half), half)
            to[j] = acc[at, :].astype(bf16)
    acc_o[...] = tn(c0[...], g0[...])
    for c, g in ((c1, g1), (c2, g2), (c3, g3)):
        acc_o[...] += tn(c[...], g[...])
    for to, which in ((ok, y), (os, 1 - y)):
        to[...] = acc_o[rows_of(which, half), :].astype(bf16)


def input_back_kernel(ak, ar, h, g1, gain, g_o, dg_o):
    ga = ak[...].astype(f32) + ar[...].astype(f32)
    back, dg = norm_back(h[...].astype(f32), gain[...], ga)
    g_o[...] = g1[...] + back
    dg_o[...] = dg


def loss_kernel(d_ref, live_ref, scale_ref, y, cot, t0, t1, t2, t3, bal, g_o, out_o):
    d = d_ref[0]
    rows = y.shape[0]
    aligned = jnp.zeros(y.shape, f32)
    pos = d * rows + lax.broadcasted_iota(jnp.int32, (rows, rows), 0)
    for j, t in enumerate((t0, t1, t2, t3)):
        pick = (bal[pl.ds(d ^ j, 1), :] == pos).astype(f32).astype(bf16)
        aligned = aligned + nn(pick, t[...])
    row = d * rows + lax.broadcasted_iota(jnp.int32, (rows, 1), 0)
    weight = jnp.where(row < live_ref[0], scale_ref[0], 0.0)
    out_o[...] = y[...].astype(bf16)
    g_o[...] = cot[...].astype(f32) + weight * (y[...] - aligned)


def shards(
    tokens, teacher, cotangent, lengths, balance, qkv_weight, out_weight, up_weight, down_weight,
    gains, query_scale,
):
    rows, feat = tokens.shape
    reps = lax.axis_size("rep")
    n_shard = lax.axis_size("shard")
    assert n_shard == 4
    pack = rows * n_shard
    depth = feat // n_shard
    heads = depth // HDIM
    d = lax.axis_index("shard")
    r = lax.axis_index("rep")
    d_s = jnp.reshape(d, (1,)).astype(jnp.int32)
    y_bit = r & 1
    y_s = jnp.reshape(y_bit, (1,)).astype(jnp.int32)

    def swap(x, k):
        return lax.ppermute(x, "shard", [(i, i ^ k) for i in range(n_shard)])

    def rep_swap(x, k):
        return lax.ppermute(x, "rep", [(i, i ^ k) for i in range(reps)])

    def gather(x):
        far = swap(x, 2)
        near = swap(x, 1)
        return (x, near, far, swap(far, 1))

    small = jnp.zeros((8, 384), f32)
    small = small.at[:4, :depth].set(gains.astype(f32).reshape(4, depth))
    small = small.at[4 : 4 + LAYERS, : query_scale.shape[1]].set(query_scale.astype(f32))
    rel = jnp.stack([small, swap(small, 1), swap(small, 2), swap(small, 3)])
    whole = jnp.take(rel, jnp.arange(4, dtype=jnp.int32) ^ d, axis=0)
    gain_all = whole[:, :4, :depth].transpose(1, 0, 2).reshape(LAYERS, 2, 1, feat)
    scale_raw = whole[:, 4 : 4 + LAYERS, : query_scale.shape[1]].transpose(1, 0, 2).reshape(LAYERS, HDIM)
    scale_unit = scale_base / math.sqrt(HDIM)
    head_scale = scale_unit * jnp.log1p(jnp.exp(scale_raw))
    head_rows = [jnp.tile(head_scale[l], heads).reshape(1, depth) for l in range(LAYERS)]

    seq_ends = jnp.cumsum(lengths[0])
    live = seq_ends[-1]
    positions = jnp.arange(pack, dtype=jnp.int32)
    starts = jnp.concatenate([jnp.zeros((1,), jnp.int32), seq_ends[:-1]])
    inside = positions[None, :] >= seq_ends[:, None]
    start = jnp.max(jnp.where(jnp.concatenate([jnp.ones((1, pack), bool), inside[:-1]]), starts[:, None], 0), axis=0)
    start = jnp.where(positions < live, start, positions).reshape(1, pack).astype(jnp.int32)
    count = jnp.broadcast_to(live.astype(f32), (8, 128))
    step = 1
    while step < reps:
        count = count + rep_swap(count, step)
        step *= 2
    loss_scale = (pack * reps / count[0, 0]).reshape(1)
    live_s = live.reshape(1).astype(jnp.int32)
    bal = balance.reshape(n_shard, rows)

    w_cols = (
        qkv_weight.reshape(LAYERS, depth, 3, n_shard, depth)
        .transpose(0, 3, 1, 2, 4)
        .reshape(LAYERS, n_shard, depth, 3 * depth)
    )

    def qkv_pieces(l):
        parts = [lax.dynamic_index_in_dim(w_cols[l], d ^ j, 0, keepdims=False) for j in range(4)]
        return [parts[0]] + [swap(parts[j], j) for j in (1, 2, 3)]

    tok32 = tokens.astype(f32)
    ab = (tok32 * inv_root(tok32) * gain_all[0, 0]).astype(bf16)
    state = tokens
    saved = []
    for l in range(LAYERS):
        pieces = qkv_pieces(l)
        a0, a1, a2, a3 = gather(ab)
        w_o, w_u, w_d = gather(out_weight[l]), gather(up_weight[l]), gather(down_weight[l])
        b0, b1, w_h = call(
            qkv_first_kernel,
            (d_s, a0, a1, head_rows[l], *pieces),
            [SM, VM, VM, VM, ANY, ANY, ANY, ANY],
            [sds((rows, 3 * depth), bf16)] * 2 + [sds((feat, 3 * depth), bf16)],
            [pltpu.SemaphoreType.DMA((4,))],
            flops=4 * rows * feat * 3 * depth,
            name="qkv_first",
        )
        b2, b3 = call(
            qkv_second_kernel,
            (a2, a3, head_rows[l], w_h),
            [VM] * 4,
            [sds((rows, 3 * depth), bf16)] * 2,
            flops=4 * rows * feat * 3 * depth,
            name="qkv_second",
        )
        *ctx, lse = call(
            attend_kernel,
            (d_s, b0, b1, b2, b3, start),
            [SM] + [VM] * 5,
            [sds((rows, depth), bf16)] * 4 + [sds((heads, pack), f32)],
            [pltpu.VMEM((heads, pack, HDIM), bf16)] * 3 + [pltpu.VMEM((depth, pack), f32)],
            flops=5 * pack * pack * 128 * heads,
            name="attend",
        )
        mine = [ctx[0]] + [swap(ctx[j], j) for j in (1, 2, 3)]
        h1, u, bb, hb, y, ab_next = call(
            ffn_kernel,
            (d_s, *mine, state, gain_all[l, 1], gain_all[(l + 1) % LAYERS, 0], *w_o, *w_u, *w_d),
            [SM] + [VM] * 7 + [ANY] * 12,
            [
                sds((rows, feat), f32), sds((rows, feat), f32), sds((rows, feat), bf16),
                sds((rows, feat), bf16), sds((rows, feat), f32), sds((rows, feat), bf16),
            ],
            [pltpu.VMEM((feat, feat), bf16)] * 3 + [pltpu.SemaphoreType.DMA((3, 4))],
            flops=6 * rows * feat * feat,
            name="ffn",
        )
        saved.append(dict(
            state=state, a=(a0, a1, a2, a3), w_h=w_h, b=(b0, b1, b2, b3), ctx=ctx, lse=lse,
            h1=h1, u=u, bb=bb, hb=hb, w_u=w_u, w_d=w_d,
        ))
        state, ab = y, ab_next

    g, layer_output = call(
        loss_kernel,
        (d_s, live_s, loss_scale, state, cotangent, *gather(teacher), bal),
        [SM, SM, SM] + [VM] * 7,
        [sds((rows, feat), f32), sds((rows, feat), bf16)],
        flops=2 * rows * pack * feat,
        name="loss",
    )

    z_line = reps == 8
    z_pos = r // 2
    z_inner = (z_pos == 1) | (z_pos == 2)

    def add_low(a, b):
        return (a.astype(f32) + b.astype(f32)).astype(bf16)

    def line_sum(s):
        if z_line:
            line = lambda x, pairs: lax.ppermute(
                x, "rep", [(2 * a + k, 2 * b + k) for a, b in pairs for k in range(2)]
            )
            s = add_low(s, line(s, [(0, 1), (3, 2)]))
            s = add_low(s, line(s, [(1, 2), (2, 1)]))
            back = line(s, [(1, 0), (2, 3)])
            return jnp.where(z_inner, s, back)
        k = 2
        while k < reps:
            s = add_low(s, rep_swap(s, k))
            k *= 2
        return s

    def both_halves(x):
        other = rep_swap(x, 1)
        first = jnp.where(y_bit == 0, x, other)
        second = jnp.where(y_bit == 0, other, x)
        return jnp.concatenate([first, second], axis=-2)

    results = [None] * LAYERS
    gain_parts = [[None, None] for _ in range(LAYERS)]
    scale_parts = [None] * LAYERS
    half = depth // 2
    for l in reversed(range(LAYERS)):
        sv = saved[l]
        gm, gu, g1, go, gain_parts[l][1] = call(
            ffn_back_kernel,
            (d_s, g, sv["h1"], sv["u"], gain_all[l, 1], *sv["w_u"], *sv["w_d"]),
            [SM] + [VM] * 4 + [ANY] * 8,
            [
                sds((rows, feat), bf16), sds((rows, feat), bf16), sds((rows, feat), f32),
                sds((rows, feat), bf16), sds((1, feat), f32),
            ],
            [pltpu.VMEM((feat, feat), bf16)] * 2 + [pltpu.SemaphoreType.DMA((2, 4))],
            flops=4 * rows * feat * feat,
            name="ffn_back",
        )
        go_all = gather(go)
        f_keep, f_send = call(
            ffn_grad_kernel,
            (d_s, sv["hb"], gm, sv["bb"], gu),
            [SM] + [VM] * 4,
            [sds((4, depth, feat), bf16)] * 2,
            [pltpu.VMEM((feat, feat), f32)],
            flops=4 * rows * feat * feat,
            name="ffn_grad",
        )
        f_keep, f_send = call(
            split_add_kernel, (f_keep, swap(f_send, 1)), [VM] * 2, [sds((2, depth, feat), bf16)] * 2, name="ffn_add"
        )
        f_keep, f_send = call(
            half_add_kernel, (y_s, f_keep, swap(f_send, 2)), [SM, VM, VM], [sds((2, half, feat), bf16)] * 2,
            name="ffn_half",
        )
        f_sum = add_low(f_keep, rep_swap(f_send, 1))
        f_sum = jnp.stack([line_sum(f_sum[m]) for m in range(2)])
        f_sum = both_halves(f_sum)

        *gmix, scale_parts[l] = call(
            attend_back_kernel,
            (d_s, *go_all, out_weight[l], *sv["b"], *sv["ctx"], sv["lse"], start, head_rows[l]),
            [SM] + [VM] * 16,
            [sds((rows, 3 * depth), bf16)] * 4 + [sds((1, depth), f32)],
            [pltpu.VMEM((heads, pack, HDIM), bf16)] * 4
            + [pltpu.VMEM((heads, pack), f32), pltpu.VMEM((depth, pack), f32)]
            + [pltpu.VMEM((heads, pack, HDIM), f32)] * 2,
            flops=10 * pack * pack * 128 * heads,
            name="attend_back",
        )
        a_keep, a_send = call(
            ga_kernel, (*gmix, sv["w_h"]), [VM] * 5, [sds((2, rows, feat), bf16)] * 2,
            flops=2 * pack * feat * 3 * depth, name="ga",
        )
        got = swap(a_send, 1)
        a_far = add_low(a_keep[1], got[1])
        a_near = add_low(a_keep[0], got[0])
        a_got = swap(a_far, 2)
        q_keep, q_send, o_keep, o_send = call(
            attn_grad_kernel,
            (d_s, y_s, *sv["a"], *gmix, *sv["ctx"], *go_all),
            [SM, SM] + [VM] * 16,
            [sds((4, half, 3 * depth), bf16)] * 2 + [sds((half, feat), bf16)] * 2,
            [pltpu.VMEM((feat, 3 * depth), f32), pltpu.VMEM((depth, feat), f32)],
            flops=2 * pack * feat * 4 * depth,
            name="attn_grad",
        )
        o_sum = both_halves(line_sum(add_low(o_keep, rep_swap(o_send, 1))))
        q_sum = add_low(q_keep, rep_swap(q_send, 1))
        q_sum = [line_sum(q_sum[j]) for j in range(4)]
        q_mine = jnp.stack([q_sum[0]] + [swap(q_sum[j], j) for j in (1, 2, 3)])
        q_mine = both_halves(q_mine)
        q_mine = jnp.take(q_mine, jnp.arange(4, dtype=jnp.int32) ^ d, axis=0)
        q_full = q_mine.reshape(4, depth, 3, depth).transpose(1, 2, 0, 3).reshape(depth, 3 * feat)
        results[l] = (q_full, o_sum, f_sum[0], f_sum[1])

        g, gain_parts[l][0] = call(
            input_back_kernel,
            (a_near, a_got, sv["state"], g1, gain_all[l, 0]),
            [VM] * 5,
            [sds((rows, feat), f32), sds((1, feat), f32)],
            name="input_back",
        )

    tail = jnp.concatenate(
        [gain_parts[l][k] for l in range(LAYERS) for k in range(2)]
        + [
            jnp.pad((scale_parts[l].reshape(heads, HDIM).sum(0) / head_scale[l])[None], ((0, 0), (0, feat - HDIM)))
            for l in range(LAYERS)
        ]
        + [jnp.zeros((8 - 3 * LAYERS, feat), f32)],
        axis=0,
    )
    tail = tail + swap(tail, 1)
    tail = tail + swap(tail, 2)
    step = 1
    while step < reps:
        tail = tail + rep_swap(tail, step)
        step *= 2
    grad_gains = lax.dynamic_slice_in_dim(tail[: 2 * LAYERS].reshape(LAYERS, 2, feat), d * depth, depth, axis=2)
    scale_all = tail[2 * LAYERS : 3 * LAYERS, :HDIM] * scale_unit * jax.nn.sigmoid(scale_raw)
    grad_scale = lax.dynamic_slice_in_dim(scale_all, d * (HDIM // n_shard), HDIM // n_shard, axis=1)
    stacked = [jnp.stack([results[l][k].astype(f32) for l in range(LAYERS)]) for k in range(4)]
    return (layer_output, g, stacked[0], stacked[1], stacked[2], stacked[3], grad_gains, grad_scale)


def solution(mesh):
    both = P(("rep", "shard"), None)
    in_specs = (
        both, both, both, P("rep", None), P("rep", None),
        P(None, "shard", None), P(None, "shard", None), P(None, "shard", None), P(None, "shard", None),
        P(None, None, "shard"), P(None, "shard"),
    )
    out_specs = (
        both, both,
        P(None, "shard", None), P(None, "shard", None), P(None, "shard", None), P(None, "shard", None),
        P(None, None, "shard"), P(None, "shard"),
    )
    return jax.shard_map(shards, mesh=mesh, in_specs=in_specs, out_specs=out_specs, check_vma=False)
```
